32 devices in a mesh: row: 16 (over z, x, core), col: 2 (over y).
Axes of the slice: x: 2, y: 2, z: 4, core: 2. Of those that a mesh axis runs over, the one named last changes fastest.
Arguments:
- messages: bfloat16 [32768, 512], P(('row', 'col')), may hold values from -6 to 6
- counts: int32 [512], P(('row', 'col')), may hold values from 16 to 64, as said below
- targets: int32 [32768], P(('row', 'col')), may hold values from 0 to 63
- mirror: int32 [32768], P(('row', 'col')), may hold values from 0 to 63, as said below
- atom_cot: bfloat16 [1024, 256], P(('row', 'col')), may hold values from -24 to 24
- w_self: bfloat16 [512, 512], replicated, may hold values from -0.25 to 0.25
- w_down: bfloat16 [512, 256], replicated, may hold values from -0.25 to 0.25
- w_up: bfloat16 [256, 512], replicated, may hold values from -0.375 to 0.375
- w_mlp: bfloat16 [512, 512], replicated, may hold values from -0.25 to 0.25
- w_out: bfloat16 [512, 256], replicated, may hold values from -0.25 to 0.25
Outputs:
- atoms: bfloat16 [1024, 256], P(('row', 'col'))
- grad_messages: bfloat16 [32768, 512], P(('row', 'col'))
The draws below stay inside these ranges and needn't reach their ends.
Inputs may be any that keep to these rules, and one draw needn't show every extreme that they name: counts of block (t, c, s) and block (s, c, t) are equal; diagonal blocks s = t hold an even count; in every column every target group has a block of 64 live edges. For slots k below the block's count, mirror is a one-to-one map onto the live slots of the block with target and source groups swapped in the same column, and the mirror of the mirror is k itself (in diagonal blocks no slot is its own mirror); padded slots map to themselves.
All inputs are finite; a program needn't handle non-finite values.
Results may differ from the reference program's by a relative error of at most 0.012.
Values may be sent and summed in bfloat16 or wider, within the bound.
A program may use at most 64 MiB of HBM per device.

```python
import jax
import jax.numpy as jnp
from jax import lax

DE = 512
DA = 256
DB = 256
EB = 64
ATOM_DEV = 32
GROUPS = 16
COLUMNS = 2
ATOM_G = 64
ATOMS = 1024
EDGES = 32768
N_ROW = 16
N_COL = 2


def edge_tables(key):
    base_key = jax.random.fold_in(key, 7301)
    key_off, key_diag, key_pair, key_score = jax.random.split(base_key, 4)
    group_ids = jnp.arange(N_ROW, dtype=jnp.int32)
    lower_eq = group_ids[:, None] <= group_ids[None, :]
    upper_draw = jax.random.randint(key_off, (N_COL, N_ROW, N_ROW), EB // 4, EB + 1)
    symmetric = jnp.where(lower_eq[None], upper_draw, jnp.swapaxes(upper_draw, 1, 2))
    diagonal = 2 * jax.random.randint(key_diag, (N_COL, N_ROW), EB // 8, EB // 2 + 1)
    on_diag = group_ids[:, None] == group_ids[None, :]
    symmetric = jnp.where(on_diag[None], diagonal[:, :, None], symmetric)
    row_orders = jax.vmap(lambda sub_key: jax.random.permutation(sub_key, N_ROW))(jax.random.split(key_pair, N_COL)).astype(jnp.int32)
    position = jnp.argsort(row_orders, axis=1).astype(jnp.int32)
    partner = jnp.take_along_axis(row_orders, position ^ 1, axis=1)
    full_pair = partner[:, :, None] == group_ids[None, None, :]
    counts = jnp.where(full_pair, EB, symmetric).astype(jnp.int32)
    score_raw = jax.random.randint(key_score, (N_COL, N_ROW, N_ROW, EB), 0, 65536)
    score_raw = jnp.where(lower_eq[None, :, :, None], score_raw, jnp.swapaxes(score_raw, 1, 2))
    slot_ids = jnp.arange(EB, dtype=jnp.int32)
    live_slot = slot_ids < counts[..., None]
    sort_keys = jnp.where(live_slot, score_raw * EB + slot_ids, 2 ** 24 + slot_ids)
    ordering = jnp.argsort(sort_keys, axis=-1, stable=True).astype(jnp.int32)
    inverse = jnp.argsort(ordering, axis=-1).astype(jnp.int32)
    take_pos = jnp.where(live_slot, slot_ids ^ 1, slot_ids)
    paired = jnp.take_along_axis(ordering, take_pos, axis=-1)
    involution = jnp.take_along_axis(paired, inverse, axis=-1)
    lower_tri = (group_ids[:, None] < group_ids[None, :])[None, :, :, None]
    upper_tri = (group_ids[:, None] > group_ids[None, :])[None, :, :, None]
    mirror = jnp.where(lower_tri, ordering, jnp.where(upper_tri, inverse, involution))
    return (counts.transpose(1, 0, 2).reshape(-1).astype(jnp.int32), mirror.transpose(1, 0, 2, 3).reshape(-1).astype(jnp.int32))


def draw_counts(key, part):
    return edge_tables(key)[0]


def draw_mirror(key, part):
    return edge_tables(key)[1]


def place_ends(drawn, rng, low, top_value):
    spot = [jax.random.randint(jax.random.fold_in(rng, axis), (), 0, length) for axis, length in enumerate(drawn.shape)]
    longest = drawn.shape.index(max(drawn.shape))
    next_to = spot[:longest] + [(spot[longest] + 1) % drawn.shape[longest]] + spot[longest + 1:]
    return drawn.at[tuple(spot)].set(low).at[tuple(next_to)].set(top_value)


def level_of(rng, extent, pieces, smallest, largest):
    def one(dim, blocks):
        heights = jax.random.uniform(jax.random.fold_in(jax.random.fold_in(rng, 6), dim), (blocks,), jnp.float32, smallest / len(pieces), largest / len(pieces))
        return jnp.repeat(jnp.exp(heights), extent[dim] // blocks).reshape((-1,) + (1,) * (len(extent) - dim - 1))

    gain = one(*pieces[0])
    for cut in pieces[1:]:
        gain = gain * one(*cut)
    return gain


def normal_values(own_key, dims, deviation, bound, shards=(), held_as=jnp.bfloat16):
    level = level_of(own_key, dims, shards, -0.22, 0.18) if shards else 1.0
    result = jax.random.normal(own_key, dims, jnp.float32) * deviation * level
    return jnp.minimum(jnp.maximum(result, -bound), bound).astype(held_as)


def setup_inputs(seed: int = 0) -> dict:
    keys = jax.random.split(jax.random.key(seed), 11)
    return {
        "messages": normal_values(keys[0], (EDGES, DE), 1.0, 6.0, ((0, 32),)),
        "counts": draw_counts(jax.random.fold_in(keys[10], 71), 0),
        "targets": place_ends(jax.random.randint(keys[2], (EDGES,), 0, ATOM_G), jax.random.fold_in(keys[2], 1), 0, ATOM_G - 1).astype(jnp.int32),
        "mirror": draw_mirror(jax.random.fold_in(keys[10], 71), 0),
        "atom_cot": normal_values(keys[4], (ATOMS, DA), 4.0, 24.0, ((0, 32),)),
        "w_self": normal_values(keys[5], (DE, DE), DE ** -0.5, 0.25),
        "w_down": normal_values(keys[6], (DE, DB), DE ** -0.5, 0.25),
        "w_up": normal_values(keys[7], (DB, DE), DB ** -0.5, 0.375),
        "w_mlp": normal_values(keys[8], (DE, DE), DE ** -0.5, 0.25),
        "w_out": normal_values(keys[9], (DE, DA), DE ** -0.5, 0.25),
    }


def silu_grad(values):
    sigmoid_v = jax.nn.sigmoid(values)
    return sigmoid_v * (1.0 + values * (1.0 - sigmoid_v))

def group_forward(msg_rows, mirror_rows, w_self, w_up, w_mlp):
    pre_act = jnp.dot(msg_rows, w_self, preferred_element_type=jnp.float32) + jnp.dot(mirror_rows, w_up, preferred_element_type=jnp.float32)
    first_res = (msg_rows.astype(jnp.float32) + jax.nn.silu(pre_act)).astype(jnp.bfloat16)
    pre_two = jnp.dot(first_res, w_mlp, preferred_element_type=jnp.float32)
    second_res = (first_res.astype(jnp.float32) + jax.nn.silu(pre_two)).astype(jnp.bfloat16)
    return (pre_act, pre_two, second_res)

def reference(messages, counts, targets, mirror, atom_cot, w_self, w_down, w_up, w_mlp, w_out):
    edge_ids = jnp.arange(EB * GROUPS * COLUMNS * GROUPS, dtype=jnp.int32)
    slot_ids = edge_ids % EB
    block_ids = edge_ids // EB
    source_grp = block_ids % GROUPS
    column_ids = block_ids // GROUPS % COLUMNS
    target_grp = block_ids // (GROUPS * COLUMNS)
    partner = (((source_grp * COLUMNS + column_ids) * GROUPS + target_grp) * EB + mirror).astype(jnp.int32)
    live_mask = (slot_ids < counts[block_ids]).astype(jnp.float32)
    scale_atoms = (ATOM_DEV * COLUMNS / (EB * GROUPS * COLUMNS)) ** 0.5
    atom_group = ATOM_DEV * COLUMNS
    group_edges = COLUMNS * GROUPS * EB
    down = jnp.dot(messages, w_down, preferred_element_type=jnp.float32).astype(jnp.bfloat16)
    mirrored = down[partner]

    def group_backward(msg_rows, mirror_rows, tgt_rows, live_rows, cot_rows):
        pre_act, pre_two, second_res = group_forward(msg_rows, mirror_rows, w_self, w_up, w_mlp)
        out_edge = (jnp.dot(second_res, w_out, preferred_element_type=jnp.float32) * live_rows[:, None]).astype(jnp.bfloat16)
        atom_ids = jnp.arange(atom_group, dtype=jnp.int32)
        one_hot = ((atom_ids[:, None] == tgt_rows[None, :]) & (live_rows[None, :] > 0.5)).astype(jnp.bfloat16)
        atom_rows = (jnp.dot(one_hot, out_edge, preferred_element_type=jnp.float32) * scale_atoms).astype(jnp.bfloat16)
        g_out = (cot_rows[tgt_rows].astype(jnp.float32) * scale_atoms * live_rows[:, None]).astype(jnp.bfloat16)
        g_second = jnp.dot(g_out, w_out.T, preferred_element_type=jnp.float32)
        g_pre2 = (g_second * silu_grad(pre_two)).astype(jnp.bfloat16)
        g_first = g_second + jnp.dot(g_pre2, w_mlp.T, preferred_element_type=jnp.float32)
        g_pre = (g_first * silu_grad(pre_act)).astype(jnp.bfloat16)
        return (atom_rows, g_first, g_pre)
    grouped = (messages.reshape(GROUPS, group_edges, DE), mirrored.reshape(GROUPS, group_edges, DB), targets.reshape(GROUPS, group_edges), live_mask.reshape(GROUPS, group_edges), atom_cot.reshape(GROUPS, atom_group, DA))

    def first_pass(inputs):
        atom_rows, g_first, g_pre = group_backward(*inputs)
        g_mirrored = jnp.dot(g_pre, w_up.T, preferred_element_type=jnp.float32).astype(jnp.bfloat16)
        return (atom_rows, g_mirrored)
    atoms, g_mirrored = lax.map(first_pass, grouped)
    g_down = g_mirrored.reshape(-1, DB)[partner]

    def second_pass(inputs):
        atom_rows, g_first, g_pre = group_backward(*inputs[:5])
        total = g_first + jnp.dot(g_pre, w_self.T, preferred_element_type=jnp.float32)
        total = total + jnp.dot(inputs[5], w_down.T, preferred_element_type=jnp.float32)
        return total.astype(jnp.bfloat16)
    grads = lax.map(second_pass, grouped + (g_down.reshape(GROUPS, group_edges, DB),))
    return (atoms.reshape(-1, DA), grads.reshape(-1, DE))
```

```python
import functools

import jax
import jax.numpy as jnp
from jax import lax
from jax.experimental import pallas as pl
from jax.experimental.pallas import tpu as pltpu
from jax.sharding import PartitionSpec as P

MESH = pl.DeviceIdType.MESH
F32 = jnp.float32
BF16 = jnp.bfloat16


def dot_nn(left, right):
    return jnp.dot(left, right, preferred_element_type=F32)


def dot_nt(left, right):
    return lax.dot_general(left, right, (((1,), (1,)), ((), ())), preferred_element_type=F32)


def dot_tn(left, right):
    return lax.dot_general(left, right, (((0,), (0,)), ((), ())), preferred_element_type=F32)


def sigmoid(values):
    return 0.5 + 0.5 * jnp.tanh(0.5 * values)


def partner_of(own, step, count):
    if count & (count - 1):
        return lax.rem(own + step, count)
    result = 0
    bit = 1
    while bit < count:
        mine = (own // bit) % 2
        other = (step // bit) % 2
        result = result + bit * (mine + other - 2 * mine * other)
        bit *= 2
    return result


def kernel(
    rows, cols, group, scale,
    messages, counts, targets, mirror, cot, w_self, w_down, w_up, w_mlp, w_out,
    atoms_out, grad_out,
    msg_v, targets_v, mirror_v, counts_s, cot_all, w_self_v, w_down_v, w_up_v, w_mlp_v, w_out_v,
    send_f, recv_f, send_b, recv_b, local_v, second_v, gsec_v, gpre_v, grad_v, atom_acc, atom_send, atom_recv, atoms_v,
    in_sems, out_sems, sf_sem, rf_sem, sb_sem, rb_sem, cot_ss, cot_rs, at_ss, at_rs,
):
    row = lax.axis_index("row")
    col = lax.axis_index("col")
    edge_count, _ = msg_v.shape
    block = edge_count // rows
    chunks = rows // group
    size = block * group
    atom_dev = cot.shape[0]
    atom_group = atom_dev * cols
    my_chunk = row // group
    my_in = lax.rem(row, group)

    barrier = pltpu.get_barrier_semaphore()
    for off in range(1, rows):
        pl.semaphore_signal(barrier, inc=1, device_id=(lax.rem(row + off, rows), col), device_id_type=MESH)
    for off in range(1, cols):
        pl.semaphore_signal(barrier, inc=1, device_id=(row, lax.rem(col + off, cols)), device_id_type=MESH)

    own_cot = cot_all.at[pl.ds(pl.multiple_of(col * atom_dev, atom_dev), atom_dev)]
    loads = [
        pltpu.make_async_copy(src, dst, in_sems.at[i])
        for i, (src, dst) in enumerate(
            [
                (w_down, w_down_v), (messages, msg_v), (cot, own_cot), (targets, targets_v), (counts, counts_s),
                (w_self, w_self_v), (w_out, w_out_v), (mirror, mirror_v), (w_up, w_up_v), (w_mlp, w_mlp_v),
            ]
        )
    ]
    for load in loads:
        load.start()

    def rows_of(index, length):
        return pl.ds(pl.multiple_of(index * length, length), length)

    def block_copy(src, dst, s_sems, r_sems, src_block, dst_block, sem):
        return pltpu.make_async_remote_copy(
            src_ref=src.at[rows_of(src_block, block)],
            dst_ref=dst.at[rows_of(dst_block, block)],
            send_sem=s_sems.at[src_block],
            recv_sem=r_sems.at[sem],
            device_id=(src_block, col),
            device_id_type=MESH,
        )

    def send_chunk(src, dst, s_sems, r_sems, chunk, last):
        for j in range(group - 1, -1, -1):
            other = chunk * group + partner_of(my_in, j, group)
            if j == 0:
                @pl.when(jnp.logical_not(last))
                def _():
                    block_copy(src, dst, s_sems, r_sems, other, row, row).start()
            else:
                block_copy(src, dst, s_sems, r_sems, other, row, row).start()

    def wait_chunk(src, dst, s_sems, r_sems, chunk, last):
        for j in range(group - 1, -1, -1):
            other = chunk * group + partner_of(my_in, j, group)
            if j == 0:
                @pl.when(jnp.logical_not(last))
                def _():
                    block_copy(src, dst, s_sems, r_sems, other, other, other).wait_recv()
            else:
                block_copy(src, dst, s_sems, r_sems, other, other, other).wait_recv()

    def wait_sent(src, dst, s_sems, r_sems, chunk, last):
        for j in range(group - 1, -1, -1):
            other = chunk * group + partner_of(my_in, j, group)
            if j == 0:
                @pl.when(jnp.logical_not(last))
                def _():
                    block_copy(src, dst, s_sems, r_sems, other, row, row).wait_send()
            else:
                block_copy(src, dst, s_sems, r_sems, other, row, row).wait_send()

    def chunk_at(p):
        return partner_of(my_chunk, chunks - 1 - p, chunks) if not chunks & (chunks - 1) else partner_of(my_chunk, p + 1, chunks)

    loads[0].wait()
    loads[1].wait()

    @pl.loop(0, chunks)
    def _(p):
        rows_c = rows_of(chunk_at(p), size)
        send_f[rows_c, :] = dot_nn(msg_v[rows_c, :], w_down_v[...]).astype(BF16)

    own_rows = rows_of(row, block)
    recv_f[own_rows, :] = send_f[own_rows, :]
    loads[2].wait()
    pl.semaphore_wait(barrier, rows + cols - 2)

    @pl.loop(0, chunks)
    def _(p):
        send_chunk(send_f, recv_f, sf_sem, rf_sem, chunk_at(p), p == chunks - 1)

    def cot_copy(off, owner):
        peer = lax.rem(col + off, cols)
        part = rows_of(owner, atom_dev)
        return pltpu.make_async_remote_copy(
            src_ref=cot_all.at[part],
            dst_ref=cot_all.at[part],
            send_sem=cot_ss.at[off],
            recv_sem=cot_rs.at[owner],
            device_id=(row, peer),
            device_id_type=MESH,
        )

    for off in range(1, cols):
        cot_copy(off, col).start()

    for load in loads[3:]:
        load.wait()

    @pl.loop(0, chunks)
    def _(p):
        rows_c = rows_of(chunk_at(p), size)
        local_v[rows_c, :] = dot_nn(msg_v[rows_c, :], w_self_v[...])

    for off in range(1, cols):
        cot_copy(off, lax.rem(col + off, cols)).wait_recv()
    for off in range(1, cols):
        cot_copy(off, col).wait_send()
    table = (cot_all[...].astype(F32) * scale).astype(BF16)

    def one_hot_of(chunk):
        lanes = lax.broadcasted_iota(jnp.int32, (1, size), 1)
        bound = jnp.zeros((1, size), jnp.int32)
        for j in range(group):
            bound = jnp.where(lanes // block == j, counts_s[chunk * group + j], bound)
        live = lax.rem(lanes, block) < bound
        wanted = jnp.where(live, targets_v[pl.ds(chunk, 1), :], -1)
        ids = lax.broadcasted_iota(jnp.int32, (atom_group, size), 0)
        return jnp.where(ids == wanted, 1.0, 0.0).astype(BF16)

    def mirror_of(chunk):
        lanes = lax.broadcasted_iota(jnp.int32, (1, size), 1)
        wanted = lanes // block * block + mirror_v[pl.ds(chunk, 1), :]
        ids = lax.broadcasted_iota(jnp.int32, (size, size), 0)
        return jnp.where(ids == wanted, 1.0, 0.0).astype(BF16)

    @pl.loop(0, chunks)
    def _(p):
        chunk = chunk_at(p)
        rows_c = rows_of(chunk, size)
        g_out = dot_tn(one_hot_of(chunk), table).astype(BF16)
        gsec_v[rows_c, :] = dot_nt(g_out, w_out_v[...])

    @pl.loop(0, chunks)
    def _(p):
        chunk = chunk_at(p)
        last = p == chunks - 1
        rows_c = rows_of(chunk, size)
        moves = mirror_of(chunk)
        wait_chunk(send_f, recv_f, sf_sem, rf_sem, chunk, last)
        mirrored = dot_tn(moves, recv_f[rows_c, :]).astype(BF16)
        pre_act = local_v[rows_c, :] + dot_nn(mirrored, w_up_v[...])
        q_one = sigmoid(pre_act)
        first_res = (msg_v[rows_c, :].astype(F32) + pre_act * q_one).astype(BF16)
        pre_two = dot_nn(first_res, w_mlp_v[...])
        q_two = sigmoid(pre_two)
        second_v[rows_c, :] = (first_res.astype(F32) + pre_two * q_two).astype(BF16)
        g_second = gsec_v[rows_c, :]
        g_pre2 = (g_second * (q_two * (1.0 + pre_two * (1.0 - q_two)))).astype(BF16)
        g_first = g_second + dot_nt(g_pre2, w_mlp_v[...])
        g_pre = (g_first * (q_one * (1.0 + pre_act * (1.0 - q_one)))).astype(BF16)
        g_mirrored = dot_nt(g_pre, w_up_v[...]).astype(BF16)
        send_b[rows_c, :] = dot_nn(moves, g_mirrored).astype(BF16)
        send_chunk(send_b, recv_b, sb_sem, rb_sem, chunk, last)
        local_v[rows_c, :] = g_first
        gpre_v[rows_c, :] = g_pre

    recv_b[own_rows, :] = send_b[own_rows, :]

    atom_acc[...] = jnp.zeros_like(atom_acc)

    @pl.loop(0, chunks)
    def _(p):
        chunk = chunk_at(p)
        rows_c = rows_of(chunk, size)
        out_edge = dot_nn(second_v[rows_c, :], w_out_v[...]).astype(BF16)
        atom_acc[...] += dot_nn(one_hot_of(chunk), out_edge)

    atom_send[...] = atom_acc[...].astype(BF16)

    def atom_copy(off, part, slot):
        peer = lax.rem(col + off, cols)
        return pltpu.make_async_remote_copy(
            src_ref=atom_send.at[rows_of(part, atom_dev)],
            dst_ref=atom_recv.at[rows_of(slot, atom_dev)],
            send_sem=at_ss.at[off],
            recv_sem=at_rs.at[slot],
            device_id=(row, peer),
            device_id_type=MESH,
        )

    for off in range(1, cols):
        atom_copy(off, lax.rem(col + off, cols), col).start()

    @pl.loop(0, chunks)
    def _(p):
        rows_c = rows_of(chunk_at(p), size)
        local_v[rows_c, :] += dot_nt(gpre_v[rows_c, :], w_self_v[...])

    total = atom_acc[rows_of(col, atom_dev), :]
    for off in range(1, cols):
        peer = lax.rem(col + off, cols)
        atom_copy(off, peer, peer).wait_recv()
        total = total + atom_recv[rows_of(peer, atom_dev), :].astype(F32)
    for off in range(1, cols):
        atom_copy(off, lax.rem(col + off, cols), col).wait_send()
    atoms_v[...] = (total * scale).astype(BF16)
    atoms_done = pltpu.make_async_copy(atoms_v, atoms_out, out_sems.at[chunks])
    atoms_done.start()

    def grad_copy(chunk, p):
        rows_c = rows_of(chunk, size)
        return pltpu.make_async_copy(grad_v.at[rows_c], grad_out.at[rows_c], out_sems.at[p])

    @pl.loop(0, chunks)
    def _(p):
        chunk = chunk_at(p)
        rows_c = rows_of(chunk, size)
        wait_chunk(send_b, recv_b, sb_sem, rb_sem, chunk, p == chunks - 1)
        grad_v[rows_c, :] = (local_v[rows_c, :] + dot_nt(recv_b[rows_c, :], w_down_v[...])).astype(BF16)
        grad_copy(chunk, p).start()

    @pl.loop(0, chunks)
    def _(p):
        chunk = chunk_at(p)
        wait_sent(send_f, recv_f, sf_sem, rf_sem, chunk, p == chunks - 1)
        wait_sent(send_b, recv_b, sb_sem, rb_sem, chunk, p == chunks - 1)
        grad_copy(chunk, p).wait()

    atoms_done.wait()


def on_device(messages, counts, targets, mirror, atom_cot, w_self, w_down, w_up, w_mlp, w_out):
    rows = lax.axis_size("row")
    cols = lax.axis_size("col")
    edges, de = messages.shape
    db = w_down.shape[1]
    da = w_out.shape[1]
    block = edges // rows
    group = 1
    while rows % (2 * group) == 0 and 2 * group * block <= 256:
        group *= 2
    chunks = rows // group
    size = group * block
    atom_dev = atom_cot.shape[0]
    scale = (atom_dev * cols / (edges * cols)) ** 0.5
    any_spec = pl.BlockSpec(memory_space=pl.ANY)
    dma = pltpu.SemaphoreType.DMA
    return pl.pallas_call(
        functools.partial(kernel, rows, cols, group, scale),
        out_shape=(
            jax.ShapeDtypeStruct((atom_dev, da), BF16),
            jax.ShapeDtypeStruct((edges, de), BF16),
        ),
        in_specs=[any_spec] * 10,
        out_specs=(any_spec, any_spec),
        scratch_shapes=[
            pltpu.VMEM((edges, de), BF16),
            pltpu.VMEM((chunks, size), jnp.int32),
            pltpu.VMEM((chunks, size), jnp.int32),
            pltpu.SMEM((rows,), jnp.int32),
            pltpu.VMEM((atom_dev * cols, da), BF16),
            pltpu.VMEM(w_self.shape, BF16),
            pltpu.VMEM(w_down.shape, BF16),
            pltpu.VMEM(w_up.shape, BF16),
            pltpu.VMEM(w_mlp.shape, BF16),
            pltpu.VMEM(w_out.shape, BF16),
            pltpu.VMEM((edges, db), BF16),
            pltpu.VMEM((edges, db), BF16),
            pltpu.VMEM((edges, db), BF16),
            pltpu.VMEM((edges, db), BF16),
            pltpu.VMEM((edges, de), F32),
            pltpu.VMEM((edges, de), BF16),
            pltpu.VMEM((edges, de), F32),
            pltpu.VMEM((edges, de), BF16),
            pltpu.VMEM((edges, de), BF16),
            pltpu.VMEM((atom_dev * cols, da), F32),
            pltpu.VMEM((atom_dev * cols, da), BF16),
            pltpu.VMEM((atom_dev * cols, da), BF16),
            pltpu.VMEM((atom_dev, da), BF16),
            dma((10,)),
            dma((chunks + 1,)),
            dma((rows,)),
            dma((rows,)),
            dma((rows,)),
            dma((rows,)),
            dma((cols,)),
            dma((cols,)),
            dma((cols,)),
            dma((cols,)),
        ],
        compiler_params=pltpu.CompilerParams(
            collective_id=0, has_side_effects=True, vmem_limit_bytes=60 * 1024 * 1024
        ),
    )(
        messages, counts, targets.reshape(chunks, size), mirror.reshape(chunks, size), atom_cot,
        w_self, w_down, w_up, w_mlp, w_out,
    )


def solution(mesh):
    return jax.shard_map(
        on_device,
        mesh=mesh,
        in_specs=(
            P(("row", "col"), None),
            P(("row", "col")),
            P(("row", "col")),
            P(("row", "col")),
            P(("row", "col"), None),
            P(),
            P(),
            P(),
            P(),
            P(),
        ),
        out_specs=(P(("row", "col"), None), P(("row", "col"), None)),
        check_vma=False,
    )
```

```python
import functools

import jax
import jax.numpy as jnp
from jax import lax
from jax.experimental import pallas as pl
from jax.experimental.pallas import tpu as pltpu
from jax.sharding import PartitionSpec as P

MESH = pl.DeviceIdType.MESH
F32 = jnp.float32
BF16 = jnp.bfloat16


def dot_nn(left, right):
    return jnp.dot(left, right, preferred_element_type=F32)


def dot_nt(left, right):
    return lax.dot_general(left, right, (((1,), (1,)), ((), ())), preferred_element_type=F32)


def dot_tn(left, right):
    return lax.dot_general(left, right, (((0,), (0,)), ((), ())), preferred_element_type=F32)


def sigmoid(values):
    return 0.5 + 0.5 * jnp.tanh(0.5 * values)


def partner_of(own, step, count):
    if count & (count - 1):
        return lax.rem(own + step, count)
    result = 0
    bit = 1
    while bit < count:
        mine = (own // bit) % 2
        other = (step // bit) % 2
        result = result + bit * (mine + other - 2 * mine * other)
        bit *= 2
    return result


def kernel(
    rows, cols, group, scale,
    messages, counts, targets, mirror, cot, w_self, w_down, w_up, w_mlp, w_out,
    atoms_v, grad_v,
    msg_v, targets_v, mirror_v, counts_s, cot_all, w_self_v, w_down_v, w_up_v, w_mlp_v, w_out_v,
    send_f, recv_f, send_b, recv_b, local_v, second_v, gsec_v, gpre_v, atom_acc, atom_send, atom_recv,
    in_sems, sf_sem, rf_sem, sb_sem, rb_sem, cot_ss, cot_rs, at_ss, at_rs,
):
    row = lax.axis_index("row")
    col = lax.axis_index("col")
    edge_count, _ = msg_v.shape
    block = edge_count // rows
    chunks = rows // group
    size = block * group
    atom_dev = cot.shape[0]
    atom_group = atom_dev * cols
    my_chunk = row // group
    my_in = lax.rem(row, group)

    barrier = pltpu.get_barrier_semaphore()
    for off in range(1, rows):
        pl.semaphore_signal(barrier, inc=1, device_id=(lax.rem(row + off, rows), col), device_id_type=MESH)
    for off in range(1, cols):
        pl.semaphore_signal(barrier, inc=1, device_id=(row, lax.rem(col + off, cols)), device_id_type=MESH)

    own_cot = cot_all.at[pl.ds(pl.multiple_of(col * atom_dev, atom_dev), atom_dev)]
    loads = [
        pltpu.make_async_copy(src, dst, in_sems.at[i])
        for i, (src, dst) in enumerate(
            [
                (w_down, w_down_v), (messages, msg_v), (cot, own_cot), (targets, targets_v), (counts, counts_s),
                (w_self, w_self_v), (w_out, w_out_v), (mirror, mirror_v), (w_up, w_up_v), (w_mlp, w_mlp_v),
            ]
        )
    ]
    for load in loads:
        load.start()

    def rows_of(index, length):
        return pl.ds(pl.multiple_of(index * length, length), length)

    def block_copy(src, dst, s_sems, r_sems, src_block, dst_block, sem):
        return pltpu.make_async_remote_copy(
            src_ref=src.at[rows_of(src_block, block)],
            dst_ref=dst.at[rows_of(dst_block, block)],
            send_sem=s_sems.at[src_block],
            recv_sem=r_sems.at[sem],
            device_id=(src_block, col),
            device_id_type=MESH,
        )

    def send_chunk(src, dst, s_sems, r_sems, chunk, last):
        for j in range(group - 1, -1, -1):
            other = chunk * group + partner_of(my_in, j, group)
            if j == 0:
                @pl.when(jnp.logical_not(last))
                def _():
                    block_copy(src, dst, s_sems, r_sems, other, row, row).start()
            else:
                block_copy(src, dst, s_sems, r_sems, other, row, row).start()

    def wait_chunk(src, dst, s_sems, r_sems, chunk, last):
        for j in range(group - 1, -1, -1):
            other = chunk * group + partner_of(my_in, j, group)
            if j == 0:
                @pl.when(jnp.logical_not(last))
                def _():
                    block_copy(src, dst, s_sems, r_sems, other, other, other).wait_recv()
            else:
                block_copy(src, dst, s_sems, r_sems, other, other, other).wait_recv()

    def wait_sent(src, dst, s_sems, r_sems, chunk, last):
        for j in range(group - 1, -1, -1):
            other = chunk * group + partner_of(my_in, j, group)
            if j == 0:
                @pl.when(jnp.logical_not(last))
                def _():
                    block_copy(src, dst, s_sems, r_sems, other, row, row).wait_send()
            else:
                block_copy(src, dst, s_sems, r_sems, other, row, row).wait_send()

    def chunk_at(p):
        return partner_of(my_chunk, chunks - 1 - p, chunks) if not chunks & (chunks - 1) else partner_of(my_chunk, p + 1, chunks)

    loads[0].wait()
    loads[1].wait()

    @pl.loop(0, chunks)
    def _(p):
        rows_c = rows_of(chunk_at(p), size)
        send_f[rows_c, :] = dot_nn(msg_v[rows_c, :], w_down_v[...]).astype(BF16)

    own_rows = rows_of(row, block)
    recv_f[own_rows, :] = send_f[own_rows, :]
    loads[2].wait()
    pl.semaphore_wait(barrier, rows + cols - 2)

    @pl.loop(0, chunks)
    def _(p):
        send_chunk(send_f, recv_f, sf_sem, rf_sem, chunk_at(p), p == chunks - 1)

    def cot_copy(off, owner):
        peer = lax.rem(col + off, cols)
        part = rows_of(owner, atom_dev)
        return pltpu.make_async_remote_copy(
            src_ref=cot_all.at[part],
            dst_ref=cot_all.at[part],
            send_sem=cot_ss.at[off],
            recv_sem=cot_rs.at[owner],
            device_id=(row, peer),
            device_id_type=MESH,
        )

    for off in range(1, cols):
        cot_copy(off, col).start()

    for load in loads[3:]:
        load.wait()

    @pl.loop(0, chunks)
    def _(p):
        rows_c = rows_of(chunk_at(p), size)
        local_v[rows_c, :] = dot_nn(msg_v[rows_c, :], w_self_v[...])

    for off in range(1, cols):
        cot_copy(off, lax.rem(col + off, cols)).wait_recv()
    for off in range(1, cols):
        cot_copy(off, col).wait_send()
    table = (cot_all[...].astype(F32) * scale).astype(BF16)

    def one_hot_of(chunk):
        lanes = lax.broadcasted_iota(jnp.int32, (1, size), 1)
        bound = jnp.zeros((1, size), jnp.int32)
        for j in range(group):
            bound = jnp.where(lanes // block == j, counts_s[chunk * group + j], bound)
        live = lax.rem(lanes, block) < bound
        wanted = jnp.where(live, targets_v[:, rows_of(chunk, size)], -1)
        ids = lax.broadcasted_iota(jnp.int32, (atom_group, size), 0)
        return jnp.where(ids == wanted, 1.0, 0.0).astype(BF16)

    def mirror_of(chunk):
        lanes = lax.broadcasted_iota(jnp.int32, (1, size), 1)
        wanted = lanes // block * block + mirror_v[:, rows_of(chunk, size)]
        ids = lax.broadcasted_iota(jnp.int32, (size, size), 0)
        return jnp.where(ids == wanted, 1.0, 0.0).astype(BF16)

    @pl.loop(0, chunks)
    def _(p):
        chunk = chunk_at(p)
        rows_c = rows_of(chunk, size)
        g_out = dot_tn(one_hot_of(chunk), table).astype(BF16)
        gsec_v[rows_c, :] = dot_nt(g_out, w_out_v[...])

    @pl.loop(0, chunks)
    def _(p):
        chunk = chunk_at(p)
        last = p == chunks - 1
        rows_c = rows_of(chunk, size)
        moves = mirror_of(chunk)
        wait_chunk(send_f, recv_f, sf_sem, rf_sem, chunk, last)
        mirrored = dot_tn(moves, recv_f[rows_c, :]).astype(BF16)
        pre_act = local_v[rows_c, :] + dot_nn(mirrored, w_up_v[...])
        q_one = sigmoid(pre_act)
        first_res = (msg_v[rows_c, :].astype(F32) + pre_act * q_one).astype(BF16)
        pre_two = dot_nn(first_res, w_mlp_v[...])
        q_two = sigmoid(pre_two)
        second_v[rows_c, :] = (first_res.astype(F32) + pre_two * q_two).astype(BF16)
        g_second = gsec_v[rows_c, :]
        g_pre2 = (g_second * (q_two * (1.0 + pre_two * (1.0 - q_two)))).astype(BF16)
        g_first = g_second + dot_nt(g_pre2, w_mlp_v[...])
        g_pre = (g_first * (q_one * (1.0 + pre_act * (1.0 - q_one)))).astype(BF16)
        g_mirrored = dot_nt(g_pre, w_up_v[...]).astype(BF16)
        send_b[rows_c, :] = dot_nn(moves, g_mirrored).astype(BF16)
        send_chunk(send_b, recv_b, sb_sem, rb_sem, chunk, last)
        local_v[rows_c, :] = g_first
        gpre_v[rows_c, :] = g_pre

    recv_b[own_rows, :] = send_b[own_rows, :]

    atom_acc[...] = jnp.zeros_like(atom_acc)

    @pl.loop(0, chunks)
    def _(p):
        chunk = chunk_at(p)
        rows_c = rows_of(chunk, size)
        out_edge = dot_nn(second_v[rows_c, :], w_out_v[...]).astype(BF16)
        atom_acc[...] += dot_nn(one_hot_of(chunk), out_edge)

    atom_send[...] = atom_acc[...].astype(BF16)

    def atom_copy(off, part, slot):
        peer = lax.rem(col + off, cols)
        return pltpu.make_async_remote_copy(
            src_ref=atom_send.at[rows_of(part, atom_dev)],
            dst_ref=atom_recv.at[rows_of(slot, atom_dev)],
            send_sem=at_ss.at[off],
            recv_sem=at_rs.at[slot],
            device_id=(row, peer),
            device_id_type=MESH,
        )

    for off in range(1, cols):
        atom_copy(off, lax.rem(col + off, cols), col).start()

    @pl.loop(0, chunks)
    def _(p):
        rows_c = rows_of(chunk_at(p), size)
        local_v[rows_c, :] += dot_nt(gpre_v[rows_c, :], w_self_v[...])

    total = atom_acc[rows_of(col, atom_dev), :]
    for off in range(1, cols):
        peer = lax.rem(col + off, cols)
        atom_copy(off, peer, peer).wait_recv()
        total = total + atom_recv[rows_of(peer, atom_dev), :].astype(F32)
    for off in range(1, cols):
        atom_copy(off, lax.rem(col + off, cols), col).wait_send()
    atoms_v[...] = (total * scale).astype(BF16)

    @pl.loop(0, chunks)
    def _(p):
        chunk = chunk_at(p)
        rows_c = rows_of(chunk, size)
        wait_chunk(send_b, recv_b, sb_sem, rb_sem, chunk, p == chunks - 1)
        grad_v[rows_c, :] = (local_v[rows_c, :] + dot_nt(recv_b[rows_c, :], w_down_v[...])).astype(BF16)

    @pl.loop(0, chunks)
    def _(p):
        chunk = chunk_at(p)
        wait_sent(send_f, recv_f, sf_sem, rf_sem, chunk, p == chunks - 1)
        wait_sent(send_b, recv_b, sb_sem, rb_sem, chunk, p == chunks - 1)


def on_device(messages, counts, targets, mirror, atom_cot, w_self, w_down, w_up, w_mlp, w_out):
    rows = lax.axis_size("row")
    cols = lax.axis_size("col")
    edges, de = messages.shape
    db = w_down.shape[1]
    da = w_out.shape[1]
    block = edges // rows
    group = 1
    while rows % (2 * group) == 0 and 2 * group * block <= 256:
        group *= 2
    chunks = rows // group
    size = group * block
    atom_dev = atom_cot.shape[0]
    scale = (atom_dev * cols / (edges * cols)) ** 0.5
    hbm_spec = pl.BlockSpec(memory_space=pltpu.HBM)
    vmem_spec = pl.BlockSpec(memory_space=pltpu.VMEM)
    dma = pltpu.SemaphoreType.DMA
    return pl.pallas_call(
        functools.partial(kernel, rows, cols, group, scale),
        out_shape=(pltpu.VMEM((atom_dev, da), BF16), pltpu.VMEM((edges, de), BF16)),
        in_specs=[hbm_spec] * 10,
        out_specs=(vmem_spec, vmem_spec),
        scratch_shapes=[
            pltpu.VMEM((edges, de), BF16),
            pltpu.VMEM((1, edges), jnp.int32),
            pltpu.VMEM((1, edges), jnp.int32),
            pltpu.SMEM((rows,), jnp.int32),
            pltpu.VMEM((atom_dev * cols, da), BF16),
            pltpu.VMEM(w_self.shape, BF16),
            pltpu.VMEM(w_down.shape, BF16),
            pltpu.VMEM(w_up.shape, BF16),
            pltpu.VMEM(w_mlp.shape, BF16),
            pltpu.VMEM(w_out.shape, BF16),
            pltpu.VMEM((edges, db), BF16),
            pltpu.VMEM((edges, db), BF16),
            pltpu.VMEM((edges, db), BF16),
            pltpu.VMEM((edges, db), BF16),
            pltpu.VMEM((edges, de), F32),
            pltpu.VMEM((edges, de), BF16),
            pltpu.VMEM((edges, de), F32),
            pltpu.VMEM((edges, de), BF16),
            pltpu.VMEM((atom_dev * cols, da), F32),
            pltpu.VMEM((atom_dev * cols, da), BF16),
            pltpu.VMEM((atom_dev * cols, da), BF16),
            dma((10,)),
            dma((rows,)),
            dma((rows,)),
            dma((rows,)),
            dma((rows,)),
            dma((cols,)),
            dma((cols,)),
            dma((cols,)),
            dma((cols,)),
        ],
        compiler_params=pltpu.CompilerParams(
            collective_id=0, has_side_effects=True, vmem_limit_bytes=67043328 - 2 * (edges * de + atom_dev * da) - 65536
        ),
    )(
        messages, counts, targets.reshape(1, edges), mirror.reshape(1, edges), atom_cot,
        w_self, w_down, w_up, w_mlp, w_out,
    )


def solution(mesh):
    return jax.shard_map(
        on_device,
        mesh=mesh,
        in_specs=(
            P(("row", "col"), None),
            P(("row", "col")),
            P(("row", "col")),
            P(("row", "col")),
            P(("row", "col"), None),
            P(),
            P(),
            P(),
            P(),
            P(),
        ),
        out_specs=(P(("row", "col"), None), P(("row", "col"), None)),
        check_vma=False,
    )
```

```python
import functools

import jax
import jax.numpy as jnp
from jax import lax
from jax.experimental import pallas as pl
from jax.experimental.pallas import tpu as pltpu
from jax.sharding import PartitionSpec as P

MESH = pl.DeviceIdType.MESH
F32 = jnp.float32
BF16 = jnp.bfloat16


def dot_nn(left, right):
    return jnp.dot(left, right, preferred_element_type=F32)


def dot_nt(left, right):
    return lax.dot_general(left, right, (((1,), (1,)), ((), ())), preferred_element_type=F32)


def dot_tn(left, right):
    return lax.dot_general(left, right, (((0,), (0,)), ((), ())), preferred_element_type=F32)


def sigmoid(values):
    return 0.5 + 0.5 * jnp.tanh(0.5 * values)


def partner_of(own, step, count):
    if count & (count - 1):
        return lax.rem(own + step, count)
    result = 0
    bit = 1
    while bit < count:
        mine = (own // bit) % 2
        other = (step // bit) % 2
        result = result + bit * (mine + other - 2 * mine * other)
        bit *= 2
    return result


def kernel(
    rows, cols, group, scale,
    messages, counts, targets, mirror, cot, w_self, w_down, w_up, w_mlp, w_out,
    atoms_v, grad_v,
    msg_v, targets_v, mirror_v, counts_s, cot_all, w_self_v, w_down_v, w_up_v, w_mlp_v, w_out_v,
    send_f, recv_f, send_b, recv_b, local_v, second_v, gsec_v, gpre_v, atom_acc, atom_send, atom_recv,
    in_sems, sf_sem, rf_sem, sb_sem, rb_sem, cot_ss, cot_rs, at_ss, at_rs,
):
    row = lax.axis_index("row")
    col = lax.axis_index("col")
    edge_count, _ = msg_v.shape
    block = edge_count // rows
    chunks = rows // group
    size = block * group
    atom_dev = cot.shape[0]
    atom_group = atom_dev * cols
    my_chunk = row // group
    my_in = lax.rem(row, group)

    barrier = pltpu.get_barrier_semaphore()
    for off in range(1, rows):
        pl.semaphore_signal(barrier, inc=1, device_id=(lax.rem(row + off, rows), col), device_id_type=MESH)
    for off in range(1, cols):
        pl.semaphore_signal(barrier, inc=1, device_id=(row, lax.rem(col + off, cols)), device_id_type=MESH)

    own_cot = cot_all.at[pl.ds(pl.multiple_of(col * atom_dev, atom_dev), atom_dev)]
    loads = [
        pltpu.make_async_copy(src, dst, in_sems.at[i])
        for i, (src, dst) in enumerate(
            [
                (w_down, w_down_v), (messages, msg_v), (cot, own_cot), (targets, targets_v), (counts, counts_s),
                (w_self, w_self_v), (w_out, w_out_v), (mirror, mirror_v), (w_up, w_up_v), (w_mlp, w_mlp_v),
            ]
        )
    ]
    for load in loads:
        load.start()

    def rows_of(index, length):
        return pl.ds(pl.multiple_of(index * length, length), length)

    def block_copy(src, dst, s_sems, r_sems, src_block, dst_block, sem):
        return pltpu.make_async_remote_copy(
            src_ref=src.at[rows_of(src_block, block)],
            dst_ref=dst.at[rows_of(dst_block, block)],
            send_sem=s_sems.at[src_block],
            recv_sem=r_sems.at[sem],
            device_id=(src_block, col),
            device_id_type=MESH,
        )

    def send_chunk(src, dst, s_sems, r_sems, chunk, last):
        for j in range(group - 1, -1, -1):
            other = chunk * group + partner_of(my_in, j, group)
            if j == 0:
                @pl.when(jnp.logical_not(last))
                def _():
                    block_copy(src, dst, s_sems, r_sems, other, row, row).start()
            else:
                block_copy(src, dst, s_sems, r_sems, other, row, row).start()

    def wait_chunk(src, dst, s_sems, r_sems, chunk, last):
        for j in range(group - 1, -1, -1):
            other = chunk * group + partner_of(my_in, j, group)
            if j == 0:
                @pl.when(jnp.logical_not(last))
                def _():
                    block_copy(src, dst, s_sems, r_sems, other, other, other).wait_recv()
            else:
                block_copy(src, dst, s_sems, r_sems, other, other, other).wait_recv()

    def wait_sent(src, dst, s_sems, r_sems, chunk, last):
        for j in range(group - 1, -1, -1):
            other = chunk * group + partner_of(my_in, j, group)
            if j == 0:
                @pl.when(jnp.logical_not(last))
                def _():
                    block_copy(src, dst, s_sems, r_sems, other, row, row).wait_send()
            else:
                block_copy(src, dst, s_sems, r_sems, other, row, row).wait_send()

    def picked(p, order):
        step = order[-1]
        for place, value in enumerate(order[:-1]):
            step = jnp.where(p == place, value, step)
        return step

    def chunk_at(p, order):
        return partner_of(my_chunk, picked(p, order), chunks)

    far_first = tuple(range(chunks - 1, -1, -1))
    send_order = (2, 1, 0, 3) if chunks == 4 else far_first
    work_order = (0, 1, 2, 3) if chunks == 4 else far_first
    end_order = (0, 1, 2, 3) if chunks == 4 else far_first

    loads[0].wait()
    loads[1].wait()
    loads[2].wait()
    pl.semaphore_wait(barrier, rows + cols - 2)

    @pl.loop(0, chunks)
    def _(p):
        rows_c = rows_of(chunk_at(p, send_order), size)
        send_f[rows_c, :] = dot_nn(msg_v[rows_c, :], w_down_v[...]).astype(BF16)
        send_chunk(send_f, recv_f, sf_sem, rf_sem, chunk_at(p, send_order), picked(p, send_order) == 0)

    own_rows = rows_of(row, block)
    recv_f[own_rows, :] = send_f[own_rows, :]

    def cot_copy(off, owner):
        peer = lax.rem(col + off, cols)
        part = rows_of(owner, atom_dev)
        return pltpu.make_async_remote_copy(
            src_ref=cot_all.at[part],
            dst_ref=cot_all.at[part],
            send_sem=cot_ss.at[off],
            recv_sem=cot_rs.at[owner],
            device_id=(row, peer),
            device_id_type=MESH,
        )

    for off in range(1, cols):
        cot_copy(off, col).start()

    for load in loads[3:]:
        load.wait()

    @pl.loop(0, chunks)
    def _(p):
        rows_c = rows_of(chunk_at(p, send_order), size)
        local_v[rows_c, :] = dot_nn(msg_v[rows_c, :], w_self_v[...])

    for off in range(1, cols):
        cot_copy(off, lax.rem(col + off, cols)).wait_recv()
    for off in range(1, cols):
        cot_copy(off, col).wait_send()
    table = (cot_all[...].astype(F32) * scale).astype(BF16)

    def one_hot_of(chunk):
        lanes = lax.broadcasted_iota(jnp.int32, (1, size), 1)
        bound = jnp.zeros((1, size), jnp.int32)
        for j in range(group):
            bound = jnp.where(lanes // block == j, counts_s[chunk * group + j], bound)
        live = lax.rem(lanes, block) < bound
        wanted = jnp.where(live, targets_v[:, rows_of(chunk, size)], -1)
        ids = lax.broadcasted_iota(jnp.int32, (atom_group, size), 0)
        return jnp.where(ids == wanted, 1.0, 0.0).astype(BF16)

    def mirror_of(chunk):
        lanes = lax.broadcasted_iota(jnp.int32, (1, size), 1)
        wanted = lanes // block * block + mirror_v[:, rows_of(chunk, size)]
        ids = lax.broadcasted_iota(jnp.int32, (size, size), 0)
        return jnp.where(ids == wanted, 1.0, 0.0).astype(BF16)

    @pl.loop(0, chunks)
    def _(p):
        chunk = chunk_at(p, send_order)
        rows_c = rows_of(chunk, size)
        g_out = dot_tn(one_hot_of(chunk), table).astype(BF16)
        gsec_v[rows_c, :] = dot_nt(g_out, w_out_v[...])

    @pl.loop(0, chunks)
    def _(p):
        chunk = chunk_at(p, work_order)
        last = picked(p, work_order) == 0
        rows_c = rows_of(chunk, size)
        moves = mirror_of(chunk)
        wait_chunk(send_f, recv_f, sf_sem, rf_sem, chunk, last)
        mirrored = dot_tn(moves, recv_f[rows_c, :]).astype(BF16)
        pre_act = local_v[rows_c, :] + dot_nn(mirrored, w_up_v[...])
        q_one = sigmoid(pre_act)
        first_res = (msg_v[rows_c, :].astype(F32) + pre_act * q_one).astype(BF16)
        pre_two = dot_nn(first_res, w_mlp_v[...])
        q_two = sigmoid(pre_two)
        second_v[rows_c, :] = (first_res.astype(F32) + pre_two * q_two).astype(BF16)
        g_second = gsec_v[rows_c, :]
        g_pre2 = (g_second * (q_two * (1.0 + pre_two * (1.0 - q_two)))).astype(BF16)
        g_first = g_second + dot_nt(g_pre2, w_mlp_v[...])
        g_pre = (g_first * (q_one * (1.0 + pre_act * (1.0 - q_one)))).astype(BF16)
        g_mirrored = dot_nt(g_pre, w_up_v[...]).astype(BF16)
        send_b[rows_c, :] = dot_nn(moves, g_mirrored).astype(BF16)
        send_chunk(send_b, recv_b, sb_sem, rb_sem, chunk, last)
        local_v[rows_c, :] = g_first
        gpre_v[rows_c, :] = g_pre

    recv_b[own_rows, :] = send_b[own_rows, :]

    atom_acc[...] = jnp.zeros_like(atom_acc)

    @pl.loop(0, chunks)
    def _(p):
        chunk = chunk_at(p, end_order)
        rows_c = rows_of(chunk, size)
        out_edge = dot_nn(second_v[rows_c, :], w_out_v[...]).astype(BF16)
        atom_acc[...] += dot_nn(one_hot_of(chunk), out_edge)

    atom_send[...] = atom_acc[...].astype(BF16)

    def atom_copy(off, part, slot):
        peer = lax.rem(col + off, cols)
        return pltpu.make_async_remote_copy(
            src_ref=atom_send.at[rows_of(part, atom_dev)],
            dst_ref=atom_recv.at[rows_of(slot, atom_dev)],
            send_sem=at_ss.at[off],
            recv_sem=at_rs.at[slot],
            device_id=(row, peer),
            device_id_type=MESH,
        )

    for off in range(1, cols):
        atom_copy(off, lax.rem(col + off, cols), col).start()

    @pl.loop(0, chunks)
    def _(p):
        rows_c = rows_of(chunk_at(p, end_order), size)
        local_v[rows_c, :] += dot_nt(gpre_v[rows_c, :], w_self_v[...])

    total = atom_acc[rows_of(col, atom_dev), :]
    for off in range(1, cols):
        peer = lax.rem(col + off, cols)
        atom_copy(off, peer, peer).wait_recv()
        total = total + atom_recv[rows_of(peer, atom_dev), :].astype(F32)
    for off in range(1, cols):
        atom_copy(off, lax.rem(col + off, cols), col).wait_send()
    atoms_v[...] = (total * scale).astype(BF16)

    @pl.loop(0, chunks)
    def _(p):
        chunk = chunk_at(p, end_order)
        rows_c = rows_of(chunk, size)
        wait_chunk(send_b, recv_b, sb_sem, rb_sem, chunk, picked(p, end_order) == 0)
        grad_v[rows_c, :] = (local_v[rows_c, :] + dot_nt(recv_b[rows_c, :], w_down_v[...])).astype(BF16)

    @pl.loop(0, chunks)
    def _(p):
        chunk = chunk_at(p, end_order)
        wait_sent(send_f, recv_f, sf_sem, rf_sem, chunk, picked(p, end_order) == 0)
        wait_sent(send_b, recv_b, sb_sem, rb_sem, chunk, picked(p, end_order) == 0)


def on_device(messages, counts, targets, mirror, atom_cot, w_self, w_down, w_up, w_mlp, w_out):
    rows = lax.axis_size("row")
    cols = lax.axis_size("col")
    edges, de = messages.shape
    db = w_down.shape[1]
    da = w_out.shape[1]
    block = edges // rows
    group = 1
    while rows % (2 * group) == 0 and 2 * group * block <= 256:
        group *= 2
    chunks = rows // group
    size = group * block
    atom_dev = atom_cot.shape[0]
    scale = (atom_dev * cols / (edges * cols)) ** 0.5
    hbm_spec = pl.BlockSpec(memory_space=pltpu.HBM)
    vmem_spec = pl.BlockSpec(memory_space=pltpu.VMEM)
    dma = pltpu.SemaphoreType.DMA
    return pl.pallas_call(
        functools.partial(kernel, rows, cols, group, scale),
        out_shape=(pltpu.VMEM((atom_dev, da), BF16), pltpu.VMEM((edges, de), BF16)),
        in_specs=[hbm_spec] * 10,
        out_specs=(vmem_spec, vmem_spec),
        scratch_shapes=[
            pltpu.VMEM((edges, de), BF16),
            pltpu.VMEM((1, edges), jnp.int32),
            pltpu.VMEM((1, edges), jnp.int32),
            pltpu.SMEM((rows,), jnp.int32),
            pltpu.VMEM((atom_dev * cols, da), BF16),
            pltpu.VMEM(w_self.shape, BF16),
            pltpu.VMEM(w_down.shape, BF16),
            pltpu.VMEM(w_up.shape, BF16),
            pltpu.VMEM(w_mlp.shape, BF16),
            pltpu.VMEM(w_out.shape, BF16),
            pltpu.VMEM((edges, db), BF16),
            pltpu.VMEM((edges, db), BF16),
            pltpu.VMEM((edges, db), BF16),
            pltpu.VMEM((edges, db), BF16),
            pltpu.VMEM((edges, de), F32),
            pltpu.VMEM((edges, de), BF16),
            pltpu.VMEM((edges, de), F32),
            pltpu.VMEM((edges, de), BF16),
            pltpu.VMEM((atom_dev * cols, da), F32),
            pltpu.VMEM((atom_dev * cols, da), BF16),
            pltpu.VMEM((atom_dev * cols, da), BF16),
            dma((10,)),
            dma((rows,)),
            dma((rows,)),
            dma((rows,)),
            dma((rows,)),
            dma((cols,)),
            dma((cols,)),
            dma((cols,)),
            dma((cols,)),
        ],
        compiler_params=pltpu.CompilerParams(
            collective_id=0, has_side_effects=True, vmem_limit_bytes=67043328 - 2 * (edges * de + atom_dev * da) - 65536
        ),
    )(
        messages, counts, targets.reshape(1, edges), mirror.reshape(1, edges), atom_cot,
        w_self, w_down, w_up, w_mlp, w_out,
    )


def solution(mesh):
    return jax.shard_map(
        on_device,
        mesh=mesh,
        in_specs=(
            P(("row", "col"), None),
            P(("row", "col")),
            P(("row", "col")),
            P(("row", "col")),
            P(("row", "col"), None),
            P(),
            P(),
            P(),
            P(),
            P(),
        ),
        out_specs=(P(("row", "col"), None), P(("row", "col"), None)),
        check_vma=False,
    )
```

```python
import functools

import jax
import jax.numpy as jnp
from jax import lax
from jax.experimental import pallas as pl
from jax.experimental.pallas import tpu as pltpu
from jax.sharding import PartitionSpec as P

MESH = pl.DeviceIdType.MESH
F32 = jnp.float32
BF16 = jnp.bfloat16


def dot_nn(left, right):
    return jnp.dot(left, right, preferred_element_type=F32)


def dot_nt(left, right):
    return lax.dot_general(left, right, (((1,), (1,)), ((), ())), preferred_element_type=F32)


def dot_tn(left, right):
    return lax.dot_general(left, right, (((0,), (0,)), ((), ())), preferred_element_type=F32)


def sigmoid(values):
    return 0.5 + 0.5 * jnp.tanh(0.5 * values)


def partner_of(own, step, count):
    if count & (count - 1):
        return lax.rem(own + step, count)
    result = 0
    bit = 1
    while bit < count:
        mine = (own // bit) % 2
        other = (step // bit) % 2
        result = result + bit * (mine + other - 2 * mine * other)
        bit *= 2
    return result


def kernel(
    rows, cols, group, scale,
    messages, counts, targets, mirror, cot, w_self, w_down, w_up, w_mlp, w_out,
    atoms_v, grad_v,
    msg_v, targets_v, mirror_v, counts_s, cot_all, w_self_v, w_down_v, w_up_v, w_mlp_v, w_out_v,
    send_f, recv_f, send_b, recv_b, local_v, second_v, gsec_v, gpre_v, atom_acc, atom_send, atom_recv,
    in_sems, sf_sem, rf_sem, sb_sem, rb_sem, cot_ss, cot_rs, at_ss, at_rs,
):
    row = lax.axis_index("row")
    col = lax.axis_index("col")
    edge_count, _ = msg_v.shape
    block = edge_count // rows
    chunks = rows // group
    size = block * group
    atom_dev = cot.shape[0]
    atom_group = atom_dev * cols
    my_chunk = row // group
    my_in = lax.rem(row, group)

    barrier = pltpu.get_barrier_semaphore()
    for off in range(1, rows):
        pl.semaphore_signal(barrier, inc=1, device_id=(lax.rem(row + off, rows), col), device_id_type=MESH)
    for off in range(1, cols):
        pl.semaphore_signal(barrier, inc=1, device_id=(row, lax.rem(col + off, cols)), device_id_type=MESH)

    own_cot = cot_all.at[pl.ds(pl.multiple_of(col * atom_dev, atom_dev), atom_dev)]
    loads = [
        pltpu.make_async_copy(src, dst, in_sems.at[i])
        for i, (src, dst) in enumerate(
            [
                (w_down, w_down_v), (messages, msg_v), (cot, own_cot), (targets, targets_v), (counts, counts_s),
                (w_self, w_self_v), (w_out, w_out_v), (mirror, mirror_v), (w_up, w_up_v), (w_mlp, w_mlp_v),
            ]
        )
    ]
    for load in loads:
        load.start()

    def rows_of(index, length):
        return pl.ds(pl.multiple_of(index * length, length), length)

    def block_copy(src, dst, s_sems, r_sems, src_block, dst_block, sem):
        return pltpu.make_async_remote_copy(
            src_ref=src.at[rows_of(src_block, block)],
            dst_ref=dst.at[rows_of(dst_block, block)],
            send_sem=s_sems.at[src_block],
            recv_sem=r_sems.at[sem],
            device_id=(src_block, col),
            device_id_type=MESH,
        )

    def send_chunk(src, dst, s_sems, r_sems, chunk, last):
        for j in range(group - 1, -1, -1):
            other = chunk * group + partner_of(my_in, j, group)
            if j == 0:
                @pl.when(jnp.logical_not(last))
                def _():
                    block_copy(src, dst, s_sems, r_sems, other, row, row).start()
            else:
                block_copy(src, dst, s_sems, r_sems, other, row, row).start()

    def wait_chunk(src, dst, s_sems, r_sems, chunk, last):
        for j in range(group - 1, -1, -1):
            other = chunk * group + partner_of(my_in, j, group)
            if j == 0:
                @pl.when(jnp.logical_not(last))
                def _():
                    block_copy(src, dst, s_sems, r_sems, other, other, other).wait_recv()
            else:
                block_copy(src, dst, s_sems, r_sems, other, other, other).wait_recv()

    def wait_sent(src, dst, s_sems, r_sems, chunk, last):
        for j in range(group - 1, -1, -1):
            other = chunk * group + partner_of(my_in, j, group)
            if j == 0:
                @pl.when(jnp.logical_not(last))
                def _():
                    block_copy(src, dst, s_sems, r_sems, other, row, row).wait_send()
            else:
                block_copy(src, dst, s_sems, r_sems, other, row, row).wait_send()

    def picked(p, order):
        step = order[-1]
        for place, value in enumerate(order[:-1]):
            step = jnp.where(p == place, value, step)
        return step

    def chunk_at(p, order):
        return partner_of(my_chunk, picked(p, order), chunks)

    far_first = tuple(range(chunks - 1, -1, -1))
    send_order = (2, 1, 0, 3) if chunks == 4 else far_first
    work_order = (0, 1, 2, 3) if chunks == 4 else far_first
    end_order = (0, 1, 2, 3) if chunks == 4 else far_first

    loads[0].wait()
    loads[1].wait()
    loads[2].wait()
    pl.semaphore_wait(barrier, rows + cols - 2)

    @pl.loop(0, chunks)
    def _(p):
        rows_c = rows_of(chunk_at(p, send_order), size)
        send_f[rows_c, :] = dot_nn(msg_v[rows_c, :], w_down_v[...]).astype(BF16)
        send_chunk(send_f, recv_f, sf_sem, rf_sem, chunk_at(p, send_order), picked(p, send_order) == 0)

    own_rows = rows_of(row, block)
    recv_f[own_rows, :] = send_f[own_rows, :]

    def cot_copy(off, owner):
        peer = lax.rem(col + off, cols)
        part = rows_of(owner, atom_dev)
        return pltpu.make_async_remote_copy(
            src_ref=cot_all.at[part],
            dst_ref=cot_all.at[part],
            send_sem=cot_ss.at[off],
            recv_sem=cot_rs.at[owner],
            device_id=(row, peer),
            device_id_type=MESH,
        )

    for off in range(1, cols):
        cot_copy(off, col).start()

    for load in loads[3:]:
        load.wait()

    @pl.loop(0, chunks)
    def _(p):
        rows_c = rows_of(chunk_at(p, send_order), size)
        local_v[rows_c, :] = dot_nn(msg_v[rows_c, :], w_self_v[...])

    for off in range(1, cols):
        cot_copy(off, lax.rem(col + off, cols)).wait_recv()
    for off in range(1, cols):
        cot_copy(off, col).wait_send()
    table = (cot_all[...].astype(F32) * scale).astype(BF16)

    def one_hot_of(chunk):
        lanes = lax.broadcasted_iota(jnp.int32, (1, size), 1)
        bound = jnp.zeros((1, size), jnp.int32)
        for j in range(group):
            bound = jnp.where(lanes // block == j, counts_s[chunk * group + j], bound)
        live = lax.rem(lanes, block) < bound
        wanted = jnp.where(live, targets_v[:, rows_of(chunk, size)], -1)
        ids = lax.broadcasted_iota(jnp.int32, (atom_group, size), 0)
        return jnp.where(ids == wanted, 1.0, 0.0).astype(BF16)

    def mirror_of(chunk):
        lanes = lax.broadcasted_iota(jnp.int32, (1, size), 1)
        wanted = lanes // block * block + mirror_v[:, rows_of(chunk, size)]
        ids = lax.broadcasted_iota(jnp.int32, (size, size), 0)
        return jnp.where(ids == wanted, 1.0, 0.0).astype(BF16)

    @pl.loop(0, chunks)
    def _(p):
        chunk = chunk_at(p, send_order)
        rows_c = rows_of(chunk, size)
        g_out = dot_tn(one_hot_of(chunk), table).astype(BF16)
        gsec_v[rows_c, :] = dot_nt(g_out, w_out_v[...])

    @pl.loop(0, chunks)
    def _(p):
        chunk = chunk_at(p, work_order)
        last = picked(p, work_order) == 0
        rows_c = rows_of(chunk, size)
        moves = mirror_of(chunk)
        wait_chunk(send_f, recv_f, sf_sem, rf_sem, chunk, last)
        mirrored = dot_tn(moves, recv_f[rows_c, :]).astype(BF16)
        pre_act = local_v[rows_c, :] + dot_nn(mirrored, w_up_v[...])
        q_one = sigmoid(pre_act)
        first_res = (msg_v[rows_c, :].astype(F32) + pre_act * q_one).astype(BF16)
        pre_two = dot_nn(first_res, w_mlp_v[...])
        q_two = sigmoid(pre_two)
        second_v[rows_c, :] = (first_res.astype(F32) + pre_two * q_two).astype(BF16)
        g_second = gsec_v[rows_c, :]
        g_pre2 = (g_second * (q_two * (1.0 + pre_two * (1.0 - q_two)))).astype(BF16)
        g_first = g_second + dot_nt(g_pre2, w_mlp_v[...])
        g_pre = (g_first * (q_one * (1.0 + pre_act * (1.0 - q_one)))).astype(BF16)
        g_mirrored = dot_nt(g_pre, w_up_v[...]).astype(BF16)
        send_b[rows_c, :] = dot_nn(moves, g_mirrored).astype(BF16)
        send_chunk(send_b, recv_b, sb_sem, rb_sem, chunk, last)
        local_v[rows_c, :] = g_first
        gpre_v[rows_c, :] = g_pre

    recv_b[own_rows, :] = send_b[own_rows, :]

    atom_acc[...] = jnp.zeros_like(atom_acc)

    @pl.loop(0, chunks)
    def _(p):
        chunk = chunk_at(p, end_order)
        rows_c = rows_of(chunk, size)
        out_edge = dot_nn(second_v[rows_c, :], w_out_v[...]).astype(BF16)
        atom_acc[...] += dot_nn(one_hot_of(chunk), out_edge)

    atom_send[...] = atom_acc[...].astype(BF16)

    def atom_copy(off, part, slot):
        peer = lax.rem(col + off, cols)
        return pltpu.make_async_remote_copy(
            src_ref=atom_send.at[rows_of(part, atom_dev)],
            dst_ref=atom_recv.at[rows_of(slot, atom_dev)],
            send_sem=at_ss.at[off],
            recv_sem=at_rs.at[slot],
            device_id=(row, peer),
            device_id_type=MESH,
        )

    for off in range(1, cols):
        atom_copy(off, lax.rem(col + off, cols), col).start()

    @pl.loop(0, chunks)
    def _(p):
        rows_c = rows_of(chunk_at(p, end_order), size)
        local_v[rows_c, :] += dot_nt(gpre_v[rows_c, :], w_self_v[...])

    total = atom_acc[rows_of(col, atom_dev), :]
    for off in range(1, cols):
        peer = lax.rem(col + off, cols)
        atom_copy(off, peer, peer).wait_recv()
        total = total + atom_recv[rows_of(peer, atom_dev), :].astype(F32)
    for off in range(1, cols):
        atom_copy(off, lax.rem(col + off, cols), col).wait_send()
    atoms_v[...] = (total * scale).astype(BF16)

    @pl.loop(0, chunks)
    def _(p):
        chunk = chunk_at(p, end_order)
        rows_c = rows_of(chunk, size)
        wait_chunk(send_b, recv_b, sb_sem, rb_sem, chunk, picked(p, end_order) == 0)
        grad_v[rows_c, :] = (local_v[rows_c, :] + dot_nt(recv_b[rows_c, :], w_down_v[...])).astype(BF16)

    @pl.loop(0, chunks)
    def _(p):
        chunk = chunk_at(p, end_order)
        wait_sent(send_f, recv_f, sf_sem, rf_sem, chunk, picked(p, end_order) == 0)
        wait_sent(send_b, recv_b, sb_sem, rb_sem, chunk, picked(p, end_order) == 0)


def write_out(pieces, atoms_v, grad_v, atoms_out, grad_out, sems):
    size = grad_v.shape[0] // pieces
    copies = [pltpu.make_async_copy(atoms_v, atoms_out, sems.at[pieces])]
    for i in range(pieces):
        part = pl.ds(i * size, size)
        copies.append(pltpu.make_async_copy(grad_v.at[part], grad_out.at[part], sems.at[i]))
    for copy in copies:
        copy.start()
    for copy in copies:
        copy.wait()


def on_device(messages, counts, targets, mirror, atom_cot, w_self, w_down, w_up, w_mlp, w_out):
    rows = lax.axis_size("row")
    cols = lax.axis_size("col")
    edges, de = messages.shape
    db = w_down.shape[1]
    da = w_out.shape[1]
    block = edges // rows
    group = 1
    while rows % (2 * group) == 0 and 2 * group * block <= 256:
        group *= 2
    chunks = rows // group
    size = group * block
    atom_dev = atom_cot.shape[0]
    scale = (atom_dev * cols / (edges * cols)) ** 0.5
    hbm_spec = pl.BlockSpec(memory_space=pltpu.HBM)
    vmem_spec = pl.BlockSpec(memory_space=pltpu.VMEM)
    dma = pltpu.SemaphoreType.DMA
    held = pl.pallas_call(
        functools.partial(kernel, rows, cols, group, scale),
        out_shape=(pltpu.VMEM((atom_dev, da), BF16), pltpu.VMEM((edges, de), BF16)),
        in_specs=[hbm_spec] * 10,
        out_specs=(vmem_spec, vmem_spec),
        scratch_shapes=[
            pltpu.VMEM((edges, de), BF16),
            pltpu.VMEM((1, edges), jnp.int32),
            pltpu.VMEM((1, edges), jnp.int32),
            pltpu.SMEM((rows,), jnp.int32),
            pltpu.VMEM((atom_dev * cols, da), BF16),
            pltpu.VMEM(w_self.shape, BF16),
            pltpu.VMEM(w_down.shape, BF16),
            pltpu.VMEM(w_up.shape, BF16),
            pltpu.VMEM(w_mlp.shape, BF16),
            pltpu.VMEM(w_out.shape, BF16),
            pltpu.VMEM((edges, db), BF16),
            pltpu.VMEM((edges, db), BF16),
            pltpu.VMEM((edges, db), BF16),
            pltpu.VMEM((edges, db), BF16),
            pltpu.VMEM((edges, de), F32),
            pltpu.VMEM((edges, de), BF16),
            pltpu.VMEM((edges, de), F32),
            pltpu.VMEM((edges, de), BF16),
            pltpu.VMEM((atom_dev * cols, da), F32),
            pltpu.VMEM((atom_dev * cols, da), BF16),
            pltpu.VMEM((atom_dev * cols, da), BF16),
            dma((10,)),
            dma((rows,)),
            dma((rows,)),
            dma((rows,)),
            dma((rows,)),
            dma((cols,)),
            dma((cols,)),
            dma((cols,)),
            dma((cols,)),
        ],
        compiler_params=pltpu.CompilerParams(
            collective_id=0, has_side_effects=True, vmem_limit_bytes=67043328 - 2 * (edges * de + atom_dev * da) - 65536
        ),
    )(
        messages, counts, targets.reshape(1, edges), mirror.reshape(1, edges), atom_cot,
        w_self, w_down, w_up, w_mlp, w_out,
    )
    pieces = 8
    return pl.pallas_call(
        functools.partial(write_out, pieces),
        out_shape=(
            jax.ShapeDtypeStruct((atom_dev, da), BF16),
            jax.ShapeDtypeStruct((edges, de), BF16),
        ),
        in_specs=[pl.BlockSpec(memory_space=pl.ANY)] * 2,
        out_specs=(hbm_spec, hbm_spec),
        scratch_shapes=[dma((pieces + 1,))],
        compiler_params=pltpu.CompilerParams(vmem_limit_bytes=256 * 1024),
    )(*held)


def solution(mesh):
    return jax.shard_map(
        on_device,
        mesh=mesh,
        in_specs=(
            P(("row", "col"), None),
            P(("row", "col")),
            P(("row", "col")),
            P(("row", "col")),
            P(("row", "col"), None),
            P(),
            P(),
            P(),
            P(),
            P(),
        ),
        out_specs=(P(("row", "col"), None), P(("row", "col"), None)),
        check_vma=False,
    )
```
